256 devices in a mesh: expert: 8 (over x, y_lo), fsdp: 32 (over y_hi, z, core).
Axes of the slice: x: 4, y: 4 (y_hi: 2, y_lo: 2; y = y_hi * 2 + y_lo), z: 8, core: 2. Of those that a mesh axis runs over, the one named last changes fastest.
Arguments:
- tokens: bfloat16 [4096, 6144], P('fsdp', 'expert'), may hold values from -6 to 6
- cotangent: bfloat16 [4096, 6144], P('fsdp', 'expert'), may hold values from -6 to 6
- routed_experts: int32 [4096, 2], replicated, may hold values from 0 to 7, as said below
- route_weights: float32 [4096, 2], P('fsdp'), may hold values from 0.25 to 1
- gate_matrix: bfloat16 [6144, 32768], P(None, ('expert', 'fsdp')), may hold values from -0.078125 to 0.078125
- up_matrix: bfloat16 [6144, 32768], P(None, ('expert', 'fsdp')), may hold values from -0.078125 to 0.078125
- down_matrix: bfloat16 [32768, 6144], P(('expert', 'fsdp')), may hold values from -0.1875 to 0.1875
Outputs:
- layer_output: bfloat16 [4096, 6144], P('fsdp', 'expert')
- grad_tokens: bfloat16 [4096, 6144], P('fsdp', 'expert')
- grad_gate: bfloat16 [6144, 32768], P(None, ('expert', 'fsdp'))
- grad_up: bfloat16 [6144, 32768], P(None, ('expert', 'fsdp'))
- grad_down: bfloat16 [32768, 6144], P(('expert', 'fsdp'))
The draws below stay inside these ranges and needn't reach their ends.
Inputs may be any that keep to these rules, and one draw needn't show every extreme that they name: `routed_experts`: each row names two different experts. In every aligned block of 128 rows each expert below 2 is named by at most 16 rows; one of these experts is named by exactly 16 rows in every block, and every expert below 2 is named by exactly 16 rows in at least one block.
All inputs are finite; a program needn't handle non-finite values.
Results may differ from the reference program's by a relative error of at most 0.017.
Values may be sent and summed in bfloat16 or wider, within the bound.
No kernel may reach another device: no remote copies, remote signals or barrier semaphores. Data moves between devices by JAX's collectives and lax.ppermute only.
A program may use at most 128 MiB of HBM per device.

```python
import jax
import jax.numpy as jnp
from jax import lax

D = 6144
FF = 16384
EXPERTS = 8
WIN = 2
TOK_GRP = 128
CAP = 16
TOKENS = 4096
ROWS = 512
WFF = 32768
HD = 128


def draw_routed_experts(key, part):
    groups = TOKENS // TOK_GRP
    keylist = jax.random.split(jax.random.fold_in(key, 7), 7)
    full_expert = jax.random.randint(keylist[0], (), 0, WIN)
    counts = jax.random.randint(keylist[1], (groups, WIN), CAP // 2, CAP + 1)
    peak_block = jax.random.randint(keylist[2], (WIN,), 0, groups)
    block_index = jnp.arange(groups)[:, None]
    expert_index = jnp.arange(WIN)[None, :]
    counts = jnp.where(block_index == peak_block[None, :], CAP, counts)
    counts = jnp.where(expert_index == full_expert, CAP, counts)
    perm_keys = jax.random.split(keylist[3], groups * WIN)
    shuffles = jax.vmap(lambda subkey: jax.random.permutation(subkey, TOK_GRP))(perm_keys)
    row_ranks = jnp.argsort(shuffles, axis=1).reshape(groups, WIN, TOK_GRP)
    inside = row_ranks < counts[:, :, None]
    first_in = inside[:, 0, :].reshape(TOKENS)
    second_in = inside[:, 1, :].reshape(TOKENS)
    spare_count = EXPERTS - WIN
    other_pick = jax.random.randint(keylist[4], (TOKENS,), WIN, EXPERTS)
    other_second = WIN + (other_pick - WIN + jax.random.randint(keylist[5], (TOKENS,), 1, spare_count)) % spare_count
    pick_first = jnp.where(first_in, 0, jnp.where(second_in, 1, other_pick))
    pick_second = jnp.where(first_in & second_in, 1, jnp.where(first_in | second_in, other_pick, other_second))
    swapped = jax.random.randint(keylist[6], (TOKENS,), 0, 2)
    leading = jnp.where(swapped == 1, pick_second, pick_first)
    trailing = jnp.where(swapped == 1, pick_first, pick_second)
    return jnp.stack([leading, trailing], axis=1).astype(jnp.int32)


def with_spikes(drawn, key, source, target, blocks, factor):
    owner, partner = [(jnp.arange(drawn.shape[axis_at]) // (drawn.shape[axis_at] // blocks)).reshape([-1 if axis == axis_at else 1 for axis in range(drawn.ndim)]) for axis_at in (source, target)]
    chosen = jax.random.permutation(key, blocks)[partner]
    strong = (owner == chosen) | (owner == (partner + blocks // 2) % blocks)
    return jnp.where(strong, factor * drawn, drawn)


def block_scale(key, dims, cuts, least, top_value):
    def one(position, blocks):
        draws = jax.random.uniform(jax.random.fold_in(jax.random.fold_in(key, 6), position), (blocks,), jnp.float32, least / len(cuts), top_value / len(cuts))
        return jnp.repeat(jnp.exp(draws), dims[position] // blocks).reshape((-1,) + (1,) * (len(dims) - position - 1))

    loudness = one(*cuts[0])
    for cut in cuts[1:]:
        loudness = loudness * one(*cut)
    return loudness


def centred(key, extent, deviation, reach, shards=(), held_as=jnp.bfloat16):
    values = deviation * jax.random.normal(key, extent, jnp.float32)
    if shards:
        values = values * block_scale(key, extent, shards, -0.22, 0.18)
    return jnp.clip(values, -reach, reach).astype(held_as)


def heavy_noise(key, dims, deviation, most, pieces, heavy, kind=jnp.bfloat16):
    entries = deviation * jax.random.normal(key, dims, jnp.float32)
    if pieces:
        entries = entries * block_scale(key, dims, pieces, -0.22, 0.18)
    return jnp.clip(with_spikes(entries, jax.random.fold_in(key, 3), *heavy), -most, most).astype(kind)


def setup_inputs(seed: int = 0) -> dict:
    arg_keys = jax.random.split(jax.random.key(seed), 8)
    tokens = centred(arg_keys[0], (TOKENS, D), 1.0, 6.0, ((0, 32), (1, 8)))
    cotangent = centred(arg_keys[1], (TOKENS, D), 1.0, 6.0, ((0, 32), (1, 8)))
    routed_experts = draw_routed_experts(jax.random.fold_in(arg_keys[7], 71), 0)
    route_weights = jnp.clip(0.25 + 0.75 * jax.random.uniform(arg_keys[3], (TOKENS, 2), jnp.float32) ** block_scale(arg_keys[3], (TOKENS, 2), ((0, 32),), -0.2, 0.2), 0.25, 1.0)
    gate_matrix = centred(arg_keys[4], (D, WFF), D ** -0.5, 0.078125, ((1, 256),))
    up_matrix = centred(arg_keys[5], (D, WFF), D ** -0.5, 0.078125, ((1, 256),))
    down_matrix = heavy_noise(arg_keys[6], (WFF, D), FF ** -0.5, 0.1875, ((0, 256),), (0, 1, 256, 6.0))
    return dict(tokens=tokens, cotangent=cotangent, routed_experts=routed_experts, route_weights=route_weights, gate_matrix=gate_matrix, up_matrix=up_matrix, down_matrix=down_matrix)


def block_sums(hidden, grad_pre_gate, grad_pre_up, gate_cols, up_cols, down_rows):
    blocks = FF // HD
    zero_rows = jnp.zeros((hidden.shape[0], D), jnp.float32)

    def one_block(running, block_pos):
        first_col = (block_pos * HD).astype(jnp.int32)
        hidden_block = lax.dynamic_slice_in_dim(hidden, first_col, HD, 1)
        down_block = lax.dynamic_slice_in_dim(down_rows, first_col, HD, 0)
        gate_block = lax.dynamic_slice_in_dim(gate_cols, first_col, HD, 1)
        up_block = lax.dynamic_slice_in_dim(up_cols, first_col, HD, 1)
        dgate_block = lax.dynamic_slice_in_dim(grad_pre_gate, first_col, HD, 1)
        dup_block = lax.dynamic_slice_in_dim(grad_pre_up, first_col, HD, 1)
        out_part = jnp.dot(hidden_block, down_block, preferred_element_type=jnp.float32)
        out_part = lax.optimization_barrier(out_part.astype(jnp.bfloat16)).astype(jnp.float32)
        back_part = jnp.dot(dgate_block, gate_block.T, preferred_element_type=jnp.float32)
        back_part = back_part + jnp.dot(dup_block, up_block.T, preferred_element_type=jnp.float32)
        back_part = lax.optimization_barrier(back_part.astype(jnp.bfloat16)).astype(jnp.float32)
        return (running[0] + out_part, running[1] + back_part), None

    totals, unused = lax.scan(one_block, (zero_rows, zero_rows), jnp.arange(blocks, dtype=jnp.int32))
    return totals


def reference(tokens, cotangent, routed_experts, route_weights, gate_matrix, up_matrix, down_matrix):
    layer_sum = jnp.zeros((TOKENS, D), jnp.float32)
    back_total = jnp.zeros((TOKENS, D), jnp.float32)
    gate_grads = []
    up_grads = []
    down_grads = []
    for window_pos in range(WIN):
        hits = routed_experts == window_pos
        member = jnp.any(hits, axis=1)
        weight_all = jnp.sum(jnp.where(hits, route_weights, jnp.zeros((), jnp.float32)), axis=1)
        row_order = jnp.argsort(jnp.where(member, 0, 1).astype(jnp.int32), stable=True)[:ROWS].astype(jnp.int32)
        is_valid = member[row_order]
        token_rows = jnp.where(is_valid[:, None], tokens[row_order], jnp.zeros((), tokens.dtype))
        row_weight = jnp.where(is_valid, weight_all[row_order], jnp.zeros((), jnp.float32))
        grad_rows = (row_weight[:, None] * cotangent[row_order].astype(jnp.float32)).astype(jnp.bfloat16)
        gate_cols = gate_matrix[:, window_pos * FF:(window_pos + 1) * FF]
        up_cols = up_matrix[:, window_pos * FF:(window_pos + 1) * FF]
        down_rows = down_matrix[window_pos * FF:(window_pos + 1) * FF, :]
        pre_gate = jnp.dot(token_rows, gate_cols, preferred_element_type=jnp.float32)
        pre_up = jnp.dot(token_rows, up_cols, preferred_element_type=jnp.float32)
        sigmoid_val = jax.nn.sigmoid(pre_gate)
        activated = pre_gate * sigmoid_val
        hidden = (activated * pre_up).astype(jnp.bfloat16)
        grad_hidden = jnp.dot(grad_rows, down_rows.T, preferred_element_type=jnp.float32)
        grad_pre_gate = (grad_hidden * pre_up * (sigmoid_val * (1.0 + pre_gate * (1.0 - sigmoid_val)))).astype(jnp.bfloat16)
        grad_pre_up = (grad_hidden * activated).astype(jnp.bfloat16)
        out_sum, back_sum = block_sums(hidden, grad_pre_gate, grad_pre_up, gate_cols, up_cols, down_rows)
        layer_sum = layer_sum.at[row_order].add(jnp.where(is_valid[:, None], row_weight[:, None] * out_sum, jnp.zeros((), jnp.float32)))
        back_total = back_total.at[row_order].add(jnp.where(is_valid[:, None], back_sum, jnp.zeros((), jnp.float32)))
        gate_grads.append(jnp.dot(token_rows.T, grad_pre_gate, preferred_element_type=jnp.float32).astype(jnp.bfloat16))
        up_grads.append(jnp.dot(token_rows.T, grad_pre_up, preferred_element_type=jnp.float32).astype(jnp.bfloat16))
        down_grads.append(jnp.dot(hidden.T, grad_rows, preferred_element_type=jnp.float32).astype(jnp.bfloat16))
    return (layer_sum.astype(jnp.bfloat16), back_total.astype(jnp.bfloat16), jnp.concatenate(gate_grads, axis=1), jnp.concatenate(up_grads, axis=1), jnp.concatenate(down_grads, axis=0))
```

```python
import jax
import jax.numpy as jnp
import numpy as np
from jax import lax
from jax.experimental import pallas as pl
from jax.experimental.pallas import tpu as pltpu
from jax.sharding import Mesh, PartitionSpec as P

WIN = 2
CAP = 16
NZ = 8
AXES = ("xh", "xl", "yl", "yh", "z", "core")
INTERPRET = False
F32 = jnp.float32
BF16 = jnp.bfloat16


def swap(value, axes, bits, size):
    return lax.ppermute(value, axes, [(i, i ^ bits) for i in range(size)])


def x_swap(value, bits):
    return swap(value, ("xh", "xl"), bits, 4)


def y_swap(value, yl_bit, yh_bit):
    return swap(value, ("yl", "yh"), yl_bit * 2 + yh_bit, 4)


def core_swap(value):
    return swap(value, "core", 1, 2)


def z_step(value, step):
    return lax.ppermute(value, "z", [(i, (i + step) % NZ) for i in range(NZ)])


def z_gather(low, high):
    out_low, out_high = [None] * NZ, [None] * NZ
    out_low[0], out_high[0] = low, high
    up_low = down_low = low
    up_high = down_high = high
    for hop in range(1, 5):
        up_low = z_step(up_low, 1)
        out_low[hop] = up_low
        down_high = z_step(down_high, -1)
        out_high[NZ - hop] = down_high
        if hop < 4:
            up_high = z_step(up_high, 1)
            out_high[hop] = up_high
            down_low = z_step(down_low, -1)
            out_low[NZ - hop] = down_low
    return out_low, out_high


def add_up(*terms):
    total = terms[0].astype(F32)
    for term in terms[1:]:
        total = total + term.astype(F32)
    return total.astype(BF16)


def z_reduce(low, high):
    down_low = z_step(add_up(*low(4)), -1)
    up_high = z_step(add_up(*high(4)), 1)
    down_high = z_step(add_up(*high(3)), -1)
    up_low = z_step(add_up(*low(5)), 1)
    for dz in (3, 2, 1):
        down_low = z_step(add_up(*low(dz), down_low), -1)
        up_high = z_step(add_up(*high(NZ - dz), up_high), 1)
        if dz > 1:
            down_high = z_step(add_up(*high(dz - 1), down_high), -1)
            up_low = z_step(add_up(*low(NZ + 1 - dz), up_low), 1)
    return [*low(0), down_low, up_low], [*high(0), down_high, up_high]


def rows_of(ref, order):
    parts = []
    for dc in range(2):
        for dz in range(NZ):
            for dyh in range(2):
                parts.append(ref[dc, dz, 0, dyh, 0] if order == "z" else ref[dc, 0, dyh, dz, 0])
    return jnp.concatenate(parts, axis=0)


def pre_kernel(flip, tok, grd, gate, up, down, hid, gp, acc, acc_grad):
    step = pl.program_id(0)

    @pl.when(step == 0)
    def _():
        acc[...] = jnp.zeros_like(acc)
        acc_grad[...] = jnp.zeros_like(acc_grad)

    weights = jnp.concatenate([gate[...], up[...]], axis=1)
    acc[...] += jnp.dot(rows_of(tok, "z"), weights, preferred_element_type=F32)
    acc_grad[...] += lax.dot_general(
        rows_of(grd, "y"), down[...], (((1,), (1,)), ((), ())), preferred_element_type=F32
    )

    @pl.when(step == pl.num_programs(0) - 1)
    def _():
        width = hid.shape[1]
        pre_gate = acc[:, :width]
        pre_up = acc[:, width:]
        grad_hidden = acc_grad[...]
        sig = jax.nn.sigmoid(pre_gate)
        act = pre_gate * sig
        hid[...] = (act * pre_up).astype(BF16)
        gp[:, :width] = (grad_hidden * pre_up * (sig * (1.0 + pre_gate * (1.0 - sig)))).astype(BF16)
        gp[:, width:] = (grad_hidden * act).astype(BF16)


def post_kernel(flip, tok, grd, gate, up, down, hid, gp, out0, out1, back0, back1, gg, gu, gd):
    width = hid.shape[1]
    hidden = hid[...]
    grads = gp[...]
    weights = jnp.concatenate([gate[...], up[...]], axis=1)
    out_part = jnp.dot(hidden, down[...], preferred_element_type=F32).astype(BF16)
    back_part = lax.dot_general(
        grads, weights, (((1,), (1,)), ((), ())), preferred_element_type=F32
    ).astype(BF16)
    at = 0
    for out_ref, back_ref in ((out0, back0), (out1, back1)):
        for dz in range(NZ):
            for dyh in range(2):
                out_ref[dz, 0, dyh, 0] = out_part[at : at + CAP]
                back_ref[0, dyh, dz, 0] = back_part[at : at + CAP]
                at += CAP
    both = lax.dot_general(
        rows_of(tok, "z"), grads, (((0,), (0,)), ((), ())), preferred_element_type=F32
    ).astype(BF16)
    gg[...] = both[:, :width]
    gu[...] = both[:, width:]
    gd[...] = lax.dot_general(
        hidden, rows_of(grd, "y"), (((0,), (0,)), ((), ())), preferred_element_type=F32
    ).astype(BF16)


def local(tokens, cotangent, routed_experts, route_weights, gate, up, down):
    group_rows, width = tokens.shape
    features, hidden_width = gate.shape
    xh, xl, yl, yh, z, core = (lax.axis_index(a) for a in AXES)
    group = (yh * NZ + z) * 2 + core
    own_ids = lax.dynamic_slice_in_dim(routed_experts, group * group_rows, group_rows, 0)
    window_ids = jnp.arange(WIN, dtype=jnp.int32)
    own_hits = own_ids[:, None, :] == window_ids[None, :, None]
    member = jnp.any(own_hits, axis=2)
    count = member.astype(F32)
    earlier = (
        jnp.arange(group_rows)[:, None] > jnp.arange(group_rows)[None, :]
    ).astype(F32)
    positions = jnp.dot(earlier, count, preferred_element_type=F32).astype(jnp.int32)
    row_weight = jnp.sum(jnp.where(own_hits, route_weights[:, None, :], 0.0), axis=2)
    slots = jnp.arange(CAP, dtype=jnp.int32)
    match = member.T[:, None, :] & (positions.T[:, None, :] == slots[None, :, None])
    match = match.reshape(WIN * CAP, group_rows)
    pick = match.astype(BF16)
    slot_weight = jnp.sum(
        jnp.where(match, jnp.repeat(row_weight.T, CAP, axis=0), 0.0), axis=1
    )
    token_slots = jnp.dot(pick, tokens, preferred_element_type=F32).astype(BF16)
    grad_slots = (
        slot_weight[:, None] * jnp.dot(pick, cotangent, preferred_element_type=F32)
    ).astype(BF16)
    packed = jnp.stack(
        [token_slots.reshape(WIN, CAP, width), grad_slots.reshape(WIN, CAP, width)], axis=1
    )
    own = jnp.where(xh == 0, packed[0], packed[1])
    other = jnp.where(xh == 0, packed[1], packed[0])

    pieces = [own, x_swap(own, 1), x_swap(other, 2), x_swap(other, 3)]
    tok = jnp.stack([p[0] for p in pieces], axis=0)
    grd = jnp.stack([p[1] for p in pieces], axis=0)

    tok_low = jnp.stack([tok, y_swap(tok, 0, 1)], axis=0)
    tok_high = jnp.stack([y_swap(tok, 1, 0), y_swap(tok, 1, 1)], axis=0)
    low, high = z_gather(tok_low, tok_high)
    tok_own = jnp.stack([jnp.stack([low[dz], high[dz]], axis=0) for dz in range(NZ)], axis=0)
    tok_all = jnp.stack([tok_own, core_swap(tok_own)], axis=0)

    low, high = z_gather(grd[:2], grd[2:])
    grd_z = jnp.stack([jnp.concatenate([low[dz], high[dz]], axis=0) for dz in range(NZ)], axis=0)
    grd_p = y_swap(grd_z, 1, 0)
    grd_q = y_swap(grd_z, 1, 1)
    grd_o = jnp.concatenate(
        [y_swap(grd_q[: NZ // 2], 1, 0), y_swap(grd_p[NZ // 2 :], 1, 1)], axis=0
    )
    grd_own = jnp.stack(
        [jnp.stack([grd_z, grd_o], axis=0), jnp.stack([grd_p, grd_q], axis=0)], axis=0
    )
    grd_all = jnp.stack([grd_own, core_swap(grd_own)], axis=0)

    flip = ((xh * 2 + xl) * 2 + yl).astype(jnp.int32).reshape(1)
    rows = 2 * NZ * 2 * CAP
    tok_spec = pl.BlockSpec(
        (2, NZ, 1, 2, 1, CAP, width), lambda j, f: (0, 0, j % 2, 0, j // 2, 0, 0)
    )
    grd_spec = pl.BlockSpec(
        (2, 1, 2, NZ, 1, CAP, width), lambda j, f: (0, j % 2, 0, 0, j // 2, 0, 0)
    )
    col_spec = pl.BlockSpec((width, hidden_width), lambda j, f: (j ^ f[0], 0))
    row_spec = pl.BlockSpec((hidden_width, width), lambda j, f: (0, j ^ f[0]))
    hid_spec = pl.BlockSpec((rows, hidden_width), lambda j, f: (0, 0))
    gp_spec = pl.BlockSpec((rows, 2 * hidden_width), lambda j, f: (0, 0))
    params = pltpu.CompilerParams(
        dimension_semantics=("arbitrary",), vmem_limit_bytes=48 * 1024 * 1024
    )
    flops = 2 * rows * features * hidden_width
    moved = 2 * rows * features * 2 + 3 * features * hidden_width * 2
    hid, gp = pl.pallas_call(
        pre_kernel,
        out_shape=(
            jax.ShapeDtypeStruct((rows, hidden_width), BF16),
            jax.ShapeDtypeStruct((rows, 2 * hidden_width), BF16),
        ),
        grid_spec=pltpu.PrefetchScalarGridSpec(
            num_scalar_prefetch=1,
            grid=(8,),
            in_specs=[tok_spec, grd_spec, col_spec, col_spec, row_spec],
            out_specs=[hid_spec, gp_spec],
            scratch_shapes=[
                pltpu.VMEM((rows, 2 * hidden_width), F32),
                pltpu.VMEM((rows, hidden_width), F32),
            ],
        ),
        compiler_params=params,
        cost_estimate=pl.CostEstimate(flops=3 * flops, bytes_accessed=moved, transcendentals=0),
        interpret=INTERPRET,
        name="pre",
    )(flip, tok_all, grd_all, gate, up, down)

    out_shape = jax.ShapeDtypeStruct((NZ, 2, 2, 4, CAP, width), BF16)
    back_shape = jax.ShapeDtypeStruct((2, 2, NZ, 4, CAP, width), BF16)
    out_spec = pl.BlockSpec(
        (NZ, 1, 2, 1, CAP, width), lambda j, f: (0, j % 2, 0, j // 2, 0, 0)
    )
    back_spec = pl.BlockSpec(
        (1, 2, NZ, 1, CAP, width), lambda j, f: (j % 2, 0, 0, j // 2, 0, 0)
    )
    out0, out1, back0, back1, grad_gate, grad_up, grad_down = pl.pallas_call(
        post_kernel,
        out_shape=(
            out_shape,
            out_shape,
            back_shape,
            back_shape,
            jax.ShapeDtypeStruct(gate.shape, BF16),
            jax.ShapeDtypeStruct(up.shape, BF16),
            jax.ShapeDtypeStruct(down.shape, BF16),
        ),
        grid_spec=pltpu.PrefetchScalarGridSpec(
            num_scalar_prefetch=1,
            grid=(8,),
            in_specs=[tok_spec, grd_spec, col_spec, col_spec, row_spec, hid_spec, gp_spec],
            out_specs=[out_spec, out_spec, back_spec, back_spec, col_spec, col_spec, row_spec],
        ),
        compiler_params=params,
        cost_estimate=pl.CostEstimate(flops=6 * flops, bytes_accessed=2 * moved, transcendentals=0),
        interpret=INTERPRET,
        name="post",
    )(flip, tok_all, grd_all, gate, up, down, hid, gp)

    out_sib = core_swap(out1)
    low, high = z_reduce(
        lambda dz: [out0[dz, 0], out_sib[dz, 0]], lambda dz: [out0[dz, 1], out_sib[dz, 1]]
    )
    out_low, out_high = add_up(*low), add_up(*high)
    out_sum = add_up(
        out_low[0],
        y_swap(out_low[1], 0, 1),
        y_swap(out_high[0], 1, 0),
        y_swap(out_high[1], 1, 1),
    )

    back_sib = core_swap(back1)
    half = NZ // 2

    def back_at(dyl, dyh, part):
        return [back0[dyl, dyh][part], back_sib[dyl, dyh][part]]

    first, second = slice(0, half), slice(half, NZ)
    via_p = y_swap(add_up(*back_at(0, 1, first)), 1, 0)
    via_q = y_swap(add_up(*back_at(0, 1, second)), 1, 1)
    to_q = jnp.concatenate(
        [add_up(*back_at(1, 1, first), via_p), add_up(*back_at(1, 1, second))], axis=0
    )
    to_p = jnp.concatenate(
        [add_up(*back_at(1, 0, first)), add_up(*back_at(1, 0, second), via_q)], axis=0
    )
    back_y = add_up(*back_at(0, 0, slice(0, NZ)), y_swap(to_q, 1, 1), y_swap(to_p, 1, 0))
    low, high = z_reduce(lambda dz: [back_y[dz, :2]], lambda dz: [back_y[dz, 2:]])
    back_sum = jnp.concatenate([add_up(*low), add_up(*high)], axis=0)

    final = jnp.stack([out_sum, back_sum], axis=1)
    own_sum = final[0].astype(F32) + x_swap(final[1], 1).astype(F32)
    other_sum = x_swap(final[2], 2).astype(F32) + x_swap(final[3], 3).astype(F32)
    sums = jnp.where(
        xh == 0,
        jnp.stack([own_sum, other_sum], axis=1),
        jnp.stack([other_sum, own_sum], axis=1),
    ).reshape(2, WIN * CAP, width)
    place = match.T.astype(F32)
    weighted = jnp.where(match.T, jnp.repeat(row_weight, CAP, axis=1), 0.0)
    layer_sum = jnp.dot(
        weighted, sums[0], precision=lax.Precision.HIGHEST, preferred_element_type=F32
    )
    back_total = jnp.dot(
        place, sums[1], precision=lax.Precision.HIGHEST, preferred_element_type=F32
    )
    return (
        layer_sum.astype(BF16),
        back_total.astype(BF16),
        grad_gate,
        grad_up,
        grad_down,
    )


def solution(mesh):
    fine = Mesh(np.asarray(mesh.devices).reshape(2, 2, 2, 2, NZ, 2), AXES)
    group = ("yh", "z", "core")
    part = ("xh", "xl", "yl")
    return jax.shard_map(
        local,
        mesh=fine,
        in_specs=(
            P(group, part),
            P(group, part),
            P(),
            P(group, None),
            P(None, AXES),
            P(None, AXES),
            P(AXES, None),
        ),
        out_specs=(
            P(group, part),
            P(group, part),
            P(None, AXES),
            P(None, AXES),
            P(AXES, None),
        ),
        check_vma=False,
    )
```
